128 devices in a mesh: leaf: 4 (over x_lo, core), row: 8 (over x_hi, y), col: 4 (over z).
Axes of the slice: x: 4 (x_hi: 2, x_lo: 2; x = x_hi * 2 + x_lo), y: 4, z: 4, core: 2. Of those that a mesh axis runs over, the one named last changes fastest.
Arguments:
- parent_adj: float32 [16384, 16384], P(('leaf', 'row'), 'col'), may hold values from -70 to 70, as said below
- child_map: int32 [4, 8], replicated, may hold values from 0 to 127, as said below
- lower_panel: float32 [4, 1024, 4096], P('leaf', 'col', 'row'), may hold values from -0.09375 to 0.09375
- pivot_inverse: float32 [4, 4096, 4096], P('leaf', 'row', 'col'), may hold values from -1 to 3, as said below
Outputs:
- update_adj: float32 [4, 1024, 1024], P('leaf', 'row', 'col')
- off_adj: float32 [4, 1024, 4096], P('leaf', 'row', 'col')
- pivot_adj: float32 [4, 4096, 4096], P('leaf', 'row', 'col')
The draws below stay inside these ranges and needn't reach their ends.
Inputs may be any that keep to these rules, and one draw needn't show every extreme that they name: `child_map`: each row lists 8 distinct parent block ids in increasing order; every row contains block 0 and block 127. parent_adj is symmetric. Each pivot_inverse[c] is lower triangular with diagonal entries of 1 to 3.
All inputs are finite; a program needn't handle non-finite values.
Results may differ from the reference program's by a relative error of at most 0.0003.
Values sent between devices are 32-bit elements; how exact they have to be, the bound alone decides.
A program may use at most 128 MiB of HBM per device.

```python
import math
import jax
import jax.numpy as jnp
from jax import lax

BLK = 128
M = 16384
U = 1024
P_SIZE = 4096
NCH = 4
MB = 128
UB = 8


def draw_parent_adj(key, part):
    gaussian = jnp.clip(jax.random.normal(jax.random.fold_in(key, 3), (M, M), jnp.float32), -6.0, 6.0)
    paired = (gaussian + gaussian.T) * 0.70710678
    return paired


def draw_pivot_inverse(key, part):
    spread = jnp.clip(jax.random.normal(jax.random.fold_in(key, 7), (NCH, P_SIZE, P_SIZE), jnp.float32), -6.0, 6.0)
    diagonal = jax.random.uniform(jax.random.fold_in(key, 9), (NCH, P_SIZE), jnp.float32, 1.0, 2.0)
    lower_mask = jnp.tril(jnp.ones((P_SIZE, P_SIZE), jnp.float32), -1)
    identity = jnp.eye(P_SIZE, dtype=jnp.float32)
    return spread * lower_mask[None] / math.sqrt(P_SIZE) + diagonal[:, :, None] * identity[None]


def draw_child_map(key, part):

    def single_child(position):
        subkey = jax.random.fold_in(key, position + 17)
        shuffled = jax.random.permutation(subkey, MB - 2)[:UB - 2].astype(jnp.int32) + 1
        chosen = jnp.concatenate([jnp.zeros((1,), jnp.int32), shuffled, jnp.full((1,), MB - 1, jnp.int32)])
        return jnp.sort(chosen)
    return jax.vmap(single_child)(jnp.arange(NCH, dtype=jnp.int32))


def steps_of(stream_key, dims, split, low, top_value):
    def one(dim, shards_of):
        draws = jax.random.uniform(jax.random.fold_in(jax.random.fold_in(stream_key, 6), dim), (shards_of,), jnp.float32, low / len(split), top_value / len(split))
        return jnp.repeat(jnp.exp(draws), dims[dim] // shards_of).reshape((-1,) + (1,) * (len(dims) - dim - 1))

    gain = one(*split[0])
    for cut in split[1:]:
        gain = gain * one(*cut)
    return gain


def scatter_about(key, dims, deviation, limit, shards=(), kind=jnp.bfloat16):
    loudness = steps_of(key, dims, shards, -0.22, 0.18) if shards else 1.0
    values = jax.random.normal(key, dims, jnp.float32) * deviation * loudness
    return jnp.minimum(jnp.maximum(values, -limit), limit).astype(kind)


def setup_inputs(seed: int = 0) -> dict:
    keys = jax.random.split(jax.random.key(seed), 5)
    parent_adj = draw_parent_adj(jax.random.fold_in(keys[4], 71), 0)
    child_map = draw_child_map(jax.random.fold_in(keys[4], 71), 0)
    lower_panel = scatter_about(keys[2], (NCH, U, P_SIZE), P_SIZE ** -0.5, 0.09375, ((0, 4), (1, 4), (2, 8)), jnp.float32)
    pivot_inverse = draw_pivot_inverse(jax.random.fold_in(keys[4], 71), 0)
    return dict(parent_adj=parent_adj, child_map=child_map, lower_panel=lower_panel, pivot_inverse=pivot_inverse)


exact_mode = lax.Precision.HIGHEST


def child_pass(parent_adj, blocks, lower, inverse):
    offsets = jnp.arange(BLK, dtype=jnp.int32)
    positions = (blocks.astype(jnp.int32)[:, None] * BLK + offsets[None, :]).reshape(-1)
    selected = jnp.take(jnp.take(parent_adj, positions, axis=0), positions, axis=1)
    factor = jnp.dot(lower, inverse, precision=exact_mode, preferred_element_type=jnp.float32)
    carried = jnp.dot(selected, factor, precision=exact_mode, preferred_element_type=jnp.float32)
    pivot = jnp.dot(factor.T, carried, precision=exact_mode, preferred_element_type=jnp.float32)
    pivot = pivot + jnp.dot(inverse.T, inverse, precision=exact_mode, preferred_element_type=jnp.float32)
    return selected, -2.0 * carried, pivot


def reference(parent_adj, child_map, lower_panel, pivot_inverse):
    def single_child(packed):
        return child_pass(parent_adj, packed[0], packed[1], packed[2])

    update_adj, off_adj, pivot_adj = lax.map(single_child, (child_map, lower_panel, pivot_inverse))
    return (update_adj, off_adj, pivot_adj)
```

```python
import jax
import jax.numpy as jnp
from jax import lax
from jax.experimental import pallas as pl
from jax.experimental.pallas import tpu as pltpu
from jax.sharding import PartitionSpec as P

BLK = 128
MESH = pl.DeviceIdType.MESH
F32 = jnp.float32
BF16 = jnp.bfloat16


def split(a):
    high = a.astype(BF16)
    return high, (a - high.astype(F32)).astype(BF16)


def dot3(a_high, a_low, b_high, b_low):
    dot = lambda p, q: jnp.dot(p, q, preferred_element_type=F32)
    return dot(a_high, b_high) + (dot(a_high, b_low) + dot(a_low, b_high))


def place():
    leaf, row, col = lax.axis_index("leaf"), lax.axis_index("row"), lax.axis_index("col")
    return leaf, leaf // 2, leaf % 2, row, row // 4, row % 4, col


def neighbours():
    leaf, xl, _, row, h, y, z = place()
    return dict(
        zp=(leaf, row, (z + 1) % 4),
        zm=(leaf, row, (z + 3) % 4),
        yp=(leaf, h * 4 + (y + 1) % 4, z),
        ym=(leaf, h * 4 + (y + 3) % 4, z),
        xp=((leaf + 2) % 4, (row + 4 * xl) % 8, z),
        xm=((leaf + 2) % 4, (row + 4 * (1 - xl)) % 8, z),
        hx=(leaf, (row + 4) % 8, z),
        core=(xl * 2 + (1 - leaf % 2), row, z),
    )


class Copies:
    def __init__(self, send, recv):
        self.send, self.recv, self.count = send, recv, 0

    def make(self, src, dst, device):
        n = self.count
        self.count += 1
        return pltpu.make_async_remote_copy(
            src_ref=src, dst_ref=dst, send_sem=self.send.at[n], recv_sem=self.recv.at[n], device_id=device, device_id_type=MESH
        )


class Scatter:
    def __init__(self, copies, x, first, second, pos, plus, minus, add):
        self.x, self.first, self.second, self.pos, self.add = x, first, second, pos, add
        self.right, self.left, far = (pos + 1) % 4, (pos + 3) % 4, (pos + 2) % 4
        self.a = copies.make(x.at[far, 0], first.at[0], plus)
        self.b = copies.make(x.at[far, 1], first.at[1], minus)
        self.c = copies.make(x.at[self.right], second.at[0], plus)
        self.d = copies.make(x.at[self.left], second.at[1], minus)

    def start(self):
        self.a.start()
        self.b.start()

    def middle(self):
        self.a.wait_recv()
        self.add(self.x.at[self.right, 0], self.x.at[self.right, 0], self.first.at[0])
        self.c.start()
        self.b.wait_recv()
        self.add(self.x.at[self.left, 1], self.x.at[self.left, 1], self.first.at[1])
        self.d.start()

    def arrived(self):
        self.c.wait_recv()
        self.d.wait_recv()

    def drain(self):
        for copy in (self.a, self.b, self.c, self.d):
            copy.wait_send()


class Gather:
    def __init__(self, copies, x, pos, plus, minus, own=None):
        source = x.at[pos] if own is None else own
        right, left = (pos + 1) % 4, (pos + 3) % 4
        self.a = copies.make(source, x.at[pos], plus)
        self.b = copies.make(source, x.at[pos], minus)
        self.c = copies.make(x.at[left, 0], x.at[left, 0], plus)
        self.d = copies.make(x.at[right, 1], x.at[right, 1], minus)

    def start(self):
        self.a.start()
        self.b.start()

    def middle(self):
        self.a.wait_recv()
        self.c.start()
        self.b.wait_recv()
        self.d.start()

    def arrived(self):
        self.c.wait_recv()
        self.d.wait_recv()

    def drain(self):
        for copy in (self.a, self.b, self.c, self.d):
            copy.wait_send()


def greet(near):
    barrier = pltpu.get_barrier_semaphore()
    for device in near:
        pl.semaphore_signal(barrier, inc=1, device_id=device, device_id_type=MESH)
    pl.semaphore_wait(barrier, len(near))


def add_rows(count, step):
    def add(dst, a, b):
        def body(i, _):
            at = pl.ds(pl.multiple_of(i * step, step), step)
            dst[at, :] = a[at, :] + b[at, :]
            return 0

        lax.fori_loop(0, count // step, body, 0)

    return add


def add_tiles(dst, a, b):
    if len(dst.shape) == 2:
        dst[...] = a[...] + b[...]
        return

    def body(i, _):
        add_tiles(dst.at[i], a.at[i], b.at[i])
        return 0

    lax.fori_loop(0, dst.shape[0], body, 0)


def select_kernel(blocks, parent, out):
    leaf, _, core, row, _, _, z = place()
    owner = leaf * 8 + row
    step = pl.program_id(0)
    kind, y_to = step // 4, step % 4
    parity = jnp.where(kind == 0, core, 1 - core)

    def body(n, _):
        h_to, xl_to, j = n // 16, (n // 8) % 2, n % 8
        child = 2 * xl_to + parity
        r = blocks[child, 4 * h_to + y_to] - 4 * owner
        c = blocks[child, j] - 32 * z
        held = (r >= 0) & (r < 4) & (c >= 0) & (c < 32)
        r, c = jnp.clip(r, 0, 3), jnp.clip(c, 0, 31)
        tile = parent[pl.ds(pl.multiple_of(r * BLK, BLK), BLK), pl.ds(pl.multiple_of(c * BLK, BLK), BLK)]
        out[0, 0, n] = jnp.where(held, tile, 0.0)
        return 0

    lax.fori_loop(0, 32, body, 0)


def select(child_map, parent):
    return pl.pallas_call(
        select_kernel,
        grid=(8,),
        out_shape=jax.ShapeDtypeStruct((2, 4, 32, BLK, BLK), F32),
        in_specs=[
            pl.BlockSpec(memory_space=pltpu.SMEM),
            pl.BlockSpec(parent.shape, lambda s: (0, 0), pipeline_mode=pl.Buffered(1)),
        ],
        out_specs=pl.BlockSpec((1, 1, 32, BLK, BLK), lambda s: (s // 4, s % 4, 0, 0, 0)),
        compiler_params=pltpu.CompilerParams(vmem_limit_bytes=32 << 20),
        name="select",
    )(child_map, parent)


CHUNKS = 4


def front_kernel(
    inverse, lower, tiles,
    strips, right, mate, update, off,
    lower_all, high, low, xf, f1, f2, fx, fpair, fall,
    sib, xp, p1, p2, xq, q1, q2, xr, r1, r2, uown, uall, upair, ucat,
    send, recv, local,
):
    leaf, xl, core, row, h, y, z = place()
    near = neighbours()
    copies = Copies(send, recv)
    role = (z + 2 * h) % 4
    slot = ((role + 1) // 2) % 2
    even = z % 2 == 0
    pair = (leaf, row, jnp.where(even, (z + 1) % 4, (z + 3) % 4))
    cross = (leaf, row, jnp.where(even, (z + 3) % 4, (z + 1) % 4))
    source, upper = role < 2, h == 0
    top = source & upper
    depth, width = inverse.shape
    piece = depth // CHUNKS

    lower_gather = Gather(copies, lower_all, z, near["zp"], near["zm"], own=lower)
    to_sibling = [copies.make(tiles.at[1, (y + d) % 4], sib.at[(y + d) % 4], near["core"]) for d in (2, 1, 3, 0)]
    to_top = []
    for q in range(CHUNKS):
        at = pl.ds(q * piece, piece)
        to_top.append(copies.make(inverse.at[at], right.at[at], near["hx"]))
    swap = copies.make(inverse, mate, pair)
    rs_f = Scatter(copies, xf, f1, f2, y, near["yp"], near["ym"], add_rows(BLK, 32))
    rs_p = Scatter(copies, xp, p1, p2, y, near["yp"], near["ym"], add_tiles)
    rs_q = Scatter(copies, xq, q1, q2, 2 * h + xl, near["xp"], near["xm"], add_tiles)
    rs_r = Scatter(copies, xr, r1, r2, z, near["zp"], near["zm"], add_tiles)
    ag_f = Gather(copies, fall, y, near["yp"], near["ym"])
    ag_u = Gather(copies, uall, z, near["zp"], near["zm"])
    f_out = copies.make(fpair.at[1 - h], fx, near["hx"])
    f_back = copies.make(fall.at[y, h], fall.at[y, h], near["hx"])
    u_swap = copies.make(uall, upair, near["hx"])

    def spread(src, at_src, at):
        return (
            copies.make(src.at[at_src], strips.at[slot, at], cross),
            copies.make(src.at[at_src], strips.at[slot, at], pair),
            copies.make(strips.at[slot, at], strips.at[slot, at], pair),
        )

    spread_a = [spread(right, pl.ds(q * piece, piece), pl.ds(q * piece, piece)) for q in range(CHUNKS)]
    spread_f = [spread(fall.at[y, k], slice(None), pl.ds(depth + k * BLK, BLK)) for k in range(2)]

    def spread_start(s):
        s[0].start()
        s[1].start()

    def spread_forward(s):
        s[0].wait_recv()
        s[2].start()

    greet(list(near.values()))

    lower_here = pltpu.make_async_copy(lower, lower_all.at[z], local.at[0])
    lower_here.start()
    lower_gather.start()
    tiles_here = []
    for n, d in enumerate((2, 1, 3, 0)):
        to_sibling[n].start()
        copy = pltpu.make_async_copy(tiles.at[0, (y + d) % 4], xp.at[(y + d) % 4], local.at[1 + n])
        copy.start()
        tiles_here.append(copy)
    inverse_here = pltpu.make_async_copy(inverse, right.at[pl.ds(0, depth)], local.at[5])

    @pl.when(h == 1)
    def _():
        for copy in to_top:
            copy.start()
        inverse_here.start()

    @pl.when(top)
    def _():
        swap.start()

    def split_rows(i, _):
        at = pl.ds(pl.multiple_of(i * 32, 32), 32)
        high[at, :], low[at, :] = split(inverse[at, :])
        return 0

    lax.fori_loop(0, depth // 32, split_rows, 0)

    def sum_tiles(n):
        d = (2, 1, 3, 0)[n]
        tiles_here[n].wait()
        to_sibling[n].wait_recv()
        add_tiles(xp.at[(y + d) % 4], xp.at[(y + d) % 4], sib.at[(y + d) % 4])

    lower_gather.middle()
    sum_tiles(0)
    rs_p.start()
    lower_here.wait()
    lower_gather.arrived()

    def factor_rows(k, _):
        block = jnp.concatenate([lower_all[k, 0], lower_all[k, 1]], axis=0)
        a_high, a_low = split(block)
        product = dot3(a_high, a_low, high[...], low[...])
        xf[2 * (k % 2), k // 2] = product[:BLK]
        xf[2 * (k % 2) + 1, k // 2] = product[BLK:]
        return 0

    lax.fori_loop(0, 4, factor_rows, 0)
    rs_f.start()
    for n in (1, 2, 3):
        sum_tiles(n)
    rs_f.middle()
    rs_p.middle()

    @pl.when(h == 1)
    def _():
        inverse_here.wait()

    for q in range(CHUNKS):

        @pl.when(upper)
        def _(q=q):
            to_top[q].wait_recv()

        @pl.when(source)
        def _(q=q):
            spread_start(spread_a[q])

    rs_f.arrived()
    for k in range(2):
        add_rows(BLK, 32)(fpair.at[k], xf.at[y, k], f2.at[0, k])
        add_rows(BLK, 32)(fpair.at[k], fpair.at[k], f2.at[1, k])
    f_out.start()

    @pl.when(jnp.logical_not(source))
    def _():
        for s in spread_a:
            spread_forward(s)

    f_out.wait_recv()
    add_rows(BLK, 32)(fall.at[y, h], fpair.at[h], fx)
    f_back.start()
    f_back.wait_recv()
    ag_f.start()

    @pl.when(source)
    def _():
        for s in spread_f:
            spread_start(s)

    rs_p.arrived()
    for k in range(2):
        for x in range(2):
            for g in range(2):
                add_tiles(xq.at[2 * k + x, g], xp.at[y, k, x, g], p2.at[0, k, x, g])
                add_tiles(xq.at[2 * k + x, g], xq.at[2 * k + x, g], p2.at[1, k, x, g])
    rs_q.start()

    @pl.when(jnp.logical_not(source))
    def _():
        for s in spread_f:
            spread_forward(s)

    ag_f.middle()
    rs_q.middle()
    rs_q.arrived()
    here = 2 * h + xl
    for g in range(2):
        for k in range(4):
            xr[2 * g + k // 2, k % 2] = xq[here, g, k] + q2[0, g, k] + q2[1, g, k]
    rs_r.start()
    rs_r.middle()
    rs_r.arrived()
    for k in range(2):
        tile = xr[z, k] + r2[0, k] + r2[1, k]
        uall[z, k] = tile
        update[:, k * BLK : (k + 1) * BLK] = tile
    ag_u.start()
    ag_u.middle()
    ag_u.arrived()
    u_swap.start()
    u_swap.wait_recv()
    ag_f.arrived()
    for j in range(8):
        to = (2 * (j % 4) + j // 4) * BLK
        ucat[pl.ds(pl.multiple_of(h * BLK, BLK), BLK), to : to + BLK] = uall[j // 2, j % 2]
        ucat[pl.ds(pl.multiple_of((1 - h) * BLK, BLK), BLK), to : to + BLK] = upair[j // 2, j % 2]

    u_high, u_low = split(ucat[...])
    total = jnp.zeros((2 * BLK, width), F32)
    for k in range(4):
        f_high, f_low = split(jnp.concatenate([fall[k, 0], fall[k, 1]], axis=0))
        at = slice(2 * k * BLK, 2 * (k + 1) * BLK)
        total = total + dot3(u_high[:, at], u_low[:, at], f_high, f_low)
    right[pl.ds(depth, 2 * BLK), :] = total
    off[...] = -2.0 * right[pl.ds(pl.multiple_of(depth + h * BLK, BLK), BLK), :]

    own = pltpu.make_async_copy(right.at[pl.ds(0, depth)], strips.at[slot, pl.ds(0, depth)], local.at[6])
    own_f = [
        pltpu.make_async_copy(fall.at[y, k], strips.at[slot, pl.ds(depth + k * BLK, BLK)], local.at[7 + k]) for k in range(2)
    ]

    @pl.when(source)
    def _():
        own.start()
        for copy in own_f:
            copy.start()
        own.wait()
        for copy in own_f:
            copy.wait()

    for s in spread_a + spread_f:

        @pl.when(source)
        def _(s=s):
            s[1].wait_recv()
            s[0].wait_send()
            s[1].wait_send()

        @pl.when(jnp.logical_not(source))
        def _(s=s):
            s[2].wait_recv()
            s[2].wait_send()

    @pl.when(top)
    def _():
        swap.wait()

    @pl.when(h == 1)
    def _():
        for copy in to_top:
            copy.wait_send()

    for copy in to_sibling + [f_out, f_back, u_swap]:
        copy.wait_send()
    for group in (lower_gather, rs_f, rs_p, rs_q, rs_r, ag_f, ag_u):
        group.drain()


def front(inverse, lower, tiles):
    depth, width = inverse.shape
    tall = depth + 2 * BLK
    vmem = lambda *shape: pltpu.VMEM(shape, F32)
    tile = (BLK, BLK)
    rows = (BLK, width)
    scratch = [
        vmem(4, 2, BLK, depth),
        pltpu.VMEM((depth, width), BF16),
        pltpu.VMEM((depth, width), BF16),
        vmem(4, 2, *rows),
        vmem(2, *rows),
        vmem(2, 2, *rows),
        vmem(*rows),
        vmem(2, *rows),
        vmem(4, 2, *rows),
        vmem(4, 2, 2, 2, 4, *tile),
        vmem(4, 2, 2, 2, 4, *tile),
        vmem(2, 2, 2, 4, *tile),
        vmem(2, 2, 2, 2, 4, *tile),
        vmem(4, 2, 4, *tile),
        vmem(2, 4, *tile),
        vmem(2, 2, 4, *tile),
        vmem(4, 2, *tile),
        vmem(2, *tile),
        vmem(2, 2, *tile),
        vmem(*tile),
        vmem(4, 2, *tile),
        vmem(4, 2, *tile),
        vmem(2 * BLK, 8 * BLK),
        pltpu.SemaphoreType.DMA((64,)),
        pltpu.SemaphoreType.DMA((64,)),
        pltpu.SemaphoreType.DMA((16,)),
    ]
    whole = pl.BlockSpec(memory_space=pltpu.VMEM)
    return pl.pallas_call(
        front_kernel,
        out_shape=(
            jax.ShapeDtypeStruct((2, tall, width), F32),
            jax.ShapeDtypeStruct((tall, width), F32),
            jax.ShapeDtypeStruct((depth, width), F32),
            jax.ShapeDtypeStruct((BLK, 2 * BLK), F32),
            jax.ShapeDtypeStruct((BLK, width), F32),
        ),
        in_specs=[whole, whole, pl.BlockSpec(memory_space=pl.ANY)],
        out_specs=(whole,) * 5,
        scratch_shapes=scratch,
        compiler_params=pltpu.CompilerParams(collective_id=0, has_side_effects=True, vmem_limit_bytes=67043328),
        name="front",
    )(inverse, lower.reshape(2, BLK, depth), tiles.reshape(2, 4, 2, 2, 2, 4, *tile))


def pivot_kernel(part, out, first, second, send, recv):
    _, _, _, _, _, y, _ = place()
    near = neighbours()
    ring = (near["yp"], near["ym"])
    rows = part.shape[2]
    rs = Scatter(Copies(send, recv), part, first, second, y, *ring, add_rows(rows, 32))
    greet(list(ring))
    rs.start()
    rs.middle()
    rs.arrived()
    for k in range(2):

        def body(i, _, k=k):
            at = pl.ds(pl.multiple_of(i * 32, 32), 32)
            to = pl.ds(pl.multiple_of(i * 32 + k * rows, 32), 32)
            out[to, :] = part[y, k, at, :] + second[0, k, at, :] + second[1, k, at, :]
            return 0

        lax.fori_loop(0, rows // 32, body, 0)
    rs.drain()


def pivot_sum(part):
    _, _, rows, width = part.shape
    whole = pl.BlockSpec(memory_space=pltpu.VMEM)
    return pl.pallas_call(
        pivot_kernel,
        out_shape=jax.ShapeDtypeStruct((2 * rows, width), F32),
        in_specs=[whole],
        out_specs=whole,
        scratch_shapes=[
            pltpu.VMEM((2, rows, width), F32),
            pltpu.VMEM((2, 2, rows, width), F32),
            pltpu.SemaphoreType.DMA((4,)),
            pltpu.SemaphoreType.DMA((4,)),
        ],
        compiler_params=pltpu.CompilerParams(collective_id=1, has_side_effects=True, vmem_limit_bytes=40 << 20),
        name="pivot_sum",
    )(part)


def shards(parent_adj, child_map, lower_panel, pivot_inverse):
    inverse, lower = pivot_inverse[0], lower_panel[0]
    tiles = select(child_map, parent_adj)
    strips, right, mate, update, off = front(inverse, lower, tiles)
    high = lax.Precision.HIGH
    product = lambda w, v: jnp.einsum("skn,km->snm", w, v, precision=high, preferred_element_type=F32)
    part = product(strips, right)
    _, _, _, row, h, _, z = place()

    def with_top(part):
        first = jnp.where(z == 0, inverse, mate)
        last = jnp.where(z == 0, mate, inverse)
        return part + product(jnp.stack([first, last]), inverse)

    part = lax.cond((h == 0) & (z < 2), with_top, lambda part: part, part)
    width = part.shape[2]
    pivot = pivot_sum(part.reshape(4, 2, width // 4, width))
    return (update[None], off[None], pivot[None])


def solution(mesh):
    in_specs = (P(("leaf", "row"), "col"), P(), P("leaf", "col", "row"), P("leaf", "row", "col"))
    out_specs = (P("leaf", "row", "col"), P("leaf", "row", "col"), P("leaf", "row", "col"))
    return jax.shard_map(shards, mesh=mesh, in_specs=in_specs, out_specs=out_specs, check_vma=False)
```

```python
import jax
import jax.numpy as jnp
from jax import lax
from jax.experimental import pallas as pl
from jax.experimental.pallas import tpu as pltpu
from jax.sharding import PartitionSpec as P

BLK = 128
MESH = pl.DeviceIdType.MESH
F32 = jnp.float32
BF16 = jnp.bfloat16


def split(a):
    high = a.astype(BF16)
    return high, (a - high.astype(F32)).astype(BF16)


def dot3(a_high, a_low, b_high, b_low):
    dot = lambda p, q: jnp.dot(p, q, preferred_element_type=F32)
    return dot(a_high, b_high) + (dot(a_high, b_low) + dot(a_low, b_high))


def place():
    leaf, row, col = lax.axis_index("leaf"), lax.axis_index("row"), lax.axis_index("col")
    return leaf, leaf // 2, leaf % 2, row, row // 4, row % 4, col


def neighbours():
    leaf, xl, _, row, h, y, z = place()
    return dict(
        zp=(leaf, row, (z + 1) % 4),
        zm=(leaf, row, (z + 3) % 4),
        yp=(leaf, h * 4 + (y + 1) % 4, z),
        ym=(leaf, h * 4 + (y + 3) % 4, z),
        xp=((leaf + 2) % 4, (row + 4 * xl) % 8, z),
        xm=((leaf + 2) % 4, (row + 4 * (1 - xl)) % 8, z),
        hx=(leaf, (row + 4) % 8, z),
        core=(xl * 2 + (1 - leaf % 2), row, z),
    )


class Copies:
    def __init__(self, send, recv):
        self.send, self.recv, self.count = send, recv, 0

    def make(self, src, dst, device):
        n = self.count
        self.count += 1
        return pltpu.make_async_remote_copy(
            src_ref=src, dst_ref=dst, send_sem=self.send.at[n], recv_sem=self.recv.at[n], device_id=device, device_id_type=MESH
        )


class Scatter:
    def __init__(self, copies, x, first, second, pos, plus, minus, add):
        self.x, self.first, self.second, self.pos, self.add = x, first, second, pos, add
        self.right, self.left, far = (pos + 1) % 4, (pos + 3) % 4, (pos + 2) % 4
        self.a = copies.make(x.at[far, 0], first.at[0], plus)
        self.b = copies.make(x.at[far, 1], first.at[1], minus)
        self.c = copies.make(x.at[self.right], second.at[0], plus)
        self.d = copies.make(x.at[self.left], second.at[1], minus)

    def start(self):
        self.a.start()
        self.b.start()

    def middle(self):
        self.a.wait_recv()
        self.add(self.x.at[self.right, 0], self.x.at[self.right, 0], self.first.at[0])
        self.c.start()
        self.b.wait_recv()
        self.add(self.x.at[self.left, 1], self.x.at[self.left, 1], self.first.at[1])
        self.d.start()

    def arrived(self):
        self.c.wait_recv()
        self.d.wait_recv()

    def drain(self):
        for copy in (self.a, self.b, self.c, self.d):
            copy.wait_send()


class Gather:
    def __init__(self, copies, x, pos, plus, minus, own=None):
        source = x.at[pos] if own is None else own
        right, left = (pos + 1) % 4, (pos + 3) % 4
        self.a = copies.make(source, x.at[pos], plus)
        self.b = copies.make(source, x.at[pos], minus)
        self.c = copies.make(x.at[left, 0], x.at[left, 0], plus)
        self.d = copies.make(x.at[right, 1], x.at[right, 1], minus)

    def start(self):
        self.a.start()
        self.b.start()

    def middle(self):
        self.a.wait_recv()
        self.c.start()
        self.b.wait_recv()
        self.d.start()

    def arrived(self):
        self.c.wait_recv()
        self.d.wait_recv()

    def drain(self):
        for copy in (self.a, self.b, self.c, self.d):
            copy.wait_send()


def greet(near):
    barrier = pltpu.get_barrier_semaphore()
    for device in near:
        pl.semaphore_signal(barrier, inc=1, device_id=device, device_id_type=MESH)
    pl.semaphore_wait(barrier, len(near))


def add_rows(count, step):
    def add(dst, a, b):
        def body(i, _):
            at = pl.ds(pl.multiple_of(i * step, step), step)
            dst[at, :] = a[at, :] + b[at, :]
            return 0

        lax.fori_loop(0, count // step, body, 0)

    return add


def add_tiles(dst, a, b):
    if len(dst.shape) == 2:
        dst[...] = a[...] + b[...]
        return

    def body(i, _):
        add_tiles(dst.at[i], a.at[i], b.at[i])
        return 0

    lax.fori_loop(0, dst.shape[0], body, 0)


def select_kernel(blocks, parent, out):
    leaf, _, core, row, _, _, z = place()
    owner = leaf * 8 + row
    step = pl.program_id(0)
    kind, x_to = step // 4, step % 4
    h_to, xl_to = x_to // 2, x_to % 2
    parity = jnp.where(kind == 0, core, 1 - core)

    def body(n, _):
        y_to, j = n // 8, n % 8
        child = 2 * xl_to + parity
        r = blocks[child, 4 * h_to + y_to] - 4 * owner
        c = blocks[child, j] - 32 * z
        held = (r >= 0) & (r < 4) & (c >= 0) & (c < 32)
        r, c = jnp.clip(r, 0, 3), jnp.clip(c, 0, 31)
        tile = parent[pl.ds(pl.multiple_of(r * BLK, BLK), BLK), pl.ds(pl.multiple_of(c * BLK, BLK), BLK)]
        out[0, 0, n] = jnp.where(held, tile, 0.0)
        return 0

    lax.fori_loop(0, 32, body, 0)


def select(child_map, parent):
    return pl.pallas_call(
        select_kernel,
        grid=(8,),
        out_shape=jax.ShapeDtypeStruct((2, 4, 32, BLK, BLK), F32),
        in_specs=[
            pl.BlockSpec(memory_space=pltpu.SMEM),
            pl.BlockSpec(parent.shape, lambda s: (0, 0), pipeline_mode=pl.Buffered(1)),
        ],
        out_specs=pl.BlockSpec((1, 1, 32, BLK, BLK), lambda s: (s // 4, s % 4, 0, 0, 0)),
        compiler_params=pltpu.CompilerParams(vmem_limit_bytes=32 << 20),
        name="select",
    )(child_map, parent)


CHUNKS = 4


def front_kernel(
    inverse, lower, tiles,
    strips, right, mate, update, off,
    lower_all, high, low, xf, f1, f2, fx, fpair, fall,
    sib, xp, p1, p2, xq, q1, q2, xr, r1, r2, uown, uall, upair, ucat,
    send, recv, local,
):
    leaf, xl, core, row, h, y, z = place()
    near = neighbours()
    copies = Copies(send, recv)
    here = 2 * h + xl
    role = (z + 2 * h) % 4
    slot = ((role + 1) // 2) % 2
    even = z % 2 == 0
    pair = (leaf, row, jnp.where(even, (z + 1) % 4, (z + 3) % 4))
    cross = (leaf, row, jnp.where(even, (z + 3) % 4, (z + 1) % 4))
    source, upper = role < 2, h == 0
    top = source & upper
    depth, width = inverse.shape
    piece = depth // CHUNKS

    lower_gather = Gather(copies, lower_all, z, near["zp"], near["zm"], own=lower)
    to_sibling = [copies.make(tiles.at[1, (here + d) % 4], sib.at[(here + d) % 4], near["core"]) for d in (2, 1, 3, 0)]
    to_top = []
    for q in range(CHUNKS):
        at = pl.ds(q * piece, piece)
        to_top.append(copies.make(inverse.at[at], right.at[at], near["hx"]))
    swap = copies.make(inverse, mate, pair)
    rs_f = Scatter(copies, xf, f1, f2, y, near["yp"], near["ym"], add_rows(BLK, 32))
    rs_p = Scatter(copies, xp, p1, p2, here, near["xp"], near["xm"], add_tiles)
    rs_q = Scatter(copies, xq, q1, q2, y, near["yp"], near["ym"], add_tiles)
    rs_r = Scatter(copies, xr, r1, r2, z, near["zp"], near["zm"], add_tiles)
    ag_f = Gather(copies, fall, y, near["yp"], near["ym"])
    ag_u = Gather(copies, uall, z, near["zp"], near["zm"])
    f_out = copies.make(fpair.at[1 - h], fx, near["hx"])
    f_back = copies.make(fall.at[y, h], fall.at[y, h], near["hx"])
    u_swap = copies.make(uall, upair, near["hx"])

    def spread(src, at_src, at):
        return (
            copies.make(src.at[at_src], strips.at[slot, at], cross),
            copies.make(src.at[at_src], strips.at[slot, at], pair),
            copies.make(strips.at[slot, at], strips.at[slot, at], pair),
        )

    spread_a = [spread(right, pl.ds(q * piece, piece), pl.ds(q * piece, piece)) for q in range(CHUNKS)]
    spread_f = [spread(fall.at[y, k], slice(None), pl.ds(depth + k * BLK, BLK)) for k in range(2)]

    def spread_start(s):
        s[0].start()
        s[1].start()

    def spread_forward(s):
        s[0].wait_recv()
        s[2].start()

    greet(list(near.values()))

    lower_here = pltpu.make_async_copy(lower, lower_all.at[z], local.at[0])
    lower_here.start()
    lower_gather.start()
    tiles_here = []
    for n, d in enumerate((2, 1, 3, 0)):
        to_sibling[n].start()
        copy = pltpu.make_async_copy(tiles.at[0, (here + d) % 4], xp.at[(here + d) % 4], local.at[1 + n])
        copy.start()
        tiles_here.append(copy)
    inverse_here = pltpu.make_async_copy(inverse, right.at[pl.ds(0, depth)], local.at[5])

    @pl.when(h == 1)
    def _():
        inverse_here.start()

    @pl.when(top)
    def _():
        swap.start()

    def split_rows(i, _):
        at = pl.ds(pl.multiple_of(i * 32, 32), 32)
        high[at, :], low[at, :] = split(inverse[at, :])
        return 0

    lax.fori_loop(0, depth // 32, split_rows, 0)

    def sum_tiles(n):
        d = (2, 1, 3, 0)[n]
        tiles_here[n].wait()
        to_sibling[n].wait_recv()
        add_tiles(xp.at[(here + d) % 4], xp.at[(here + d) % 4], sib.at[(here + d) % 4])

    sum_tiles(0)
    rs_p.start()
    lower_gather.middle()
    lower_here.wait()
    lower_gather.arrived()

    @pl.when(h == 1)
    def _():
        inverse_here.wait()

    @pl.when(source & (h == 1))
    def _():
        for s in spread_a:
            spread_start(s)

    def factor_rows(k, _):
        block = jnp.concatenate([lower_all[k, 0], lower_all[k, 1]], axis=0)
        a_high, a_low = split(block)
        product = dot3(a_high, a_low, high[...], low[...])
        xf[2 * (k % 2), k // 2] = product[:BLK]
        xf[2 * (k % 2) + 1, k // 2] = product[BLK:]
        return 0

    lax.fori_loop(0, 4, factor_rows, 0)
    rs_f.start()
    for n in (1, 2, 3):
        sum_tiles(n)
    rs_p.middle()

    @pl.when(h == 1)
    def _():
        for copy in to_top:
            copy.start()

    rs_f.middle()
    rs_p.arrived()
    for k in range(2):
        for x in range(2):
            for g in range(2):
                add_tiles(xq.at[2 * k + x, g], xp.at[here, k, x, g], p2.at[0, k, x, g])
                add_tiles(xq.at[2 * k + x, g], xq.at[2 * k + x, g], p2.at[1, k, x, g])
    rs_q.start()
    rs_f.arrived()
    for k in range(2):
        add_rows(BLK, 32)(fpair.at[k], xf.at[y, k], f2.at[0, k])
        add_rows(BLK, 32)(fpair.at[k], fpair.at[k], f2.at[1, k])
    f_out.start()
    rs_q.middle()
    f_out.wait_recv()
    add_rows(BLK, 32)(fall.at[y, h], fpair.at[h], fx)
    f_back.start()
    rs_q.arrived()
    for g in range(2):
        for k in range(4):
            xr[2 * g + k // 2, k % 2] = xq[y, g, k] + q2[0, g, k] + q2[1, g, k]
    rs_r.start()
    f_back.wait_recv()
    ag_f.start()

    @pl.when(source)
    def _():
        for s in spread_f:
            spread_start(s)

    rs_r.middle()

    for q in range(CHUNKS):

        @pl.when(upper)
        def _(q=q):
            to_top[q].wait_recv()

        @pl.when(source & upper)
        def _(q=q):
            spread_start(spread_a[q])

    rs_r.arrived()
    for k in range(2):
        tile = xr[z, k] + r2[0, k] + r2[1, k]
        uall[z, k] = tile
        update[:, k * BLK : (k + 1) * BLK] = tile
    ag_u.start()
    ag_f.middle()
    ag_u.middle()

    @pl.when(jnp.logical_not(source))
    def _():
        for s in spread_f + spread_a:
            spread_forward(s)

    ag_u.arrived()
    u_swap.start()
    u_swap.wait_recv()
    ag_f.arrived()
    for j in range(8):
        to = (2 * (j % 4) + j // 4) * BLK
        ucat[pl.ds(pl.multiple_of(h * BLK, BLK), BLK), to : to + BLK] = uall[j // 2, j % 2]
        ucat[pl.ds(pl.multiple_of((1 - h) * BLK, BLK), BLK), to : to + BLK] = upair[j // 2, j % 2]

    u_high, u_low = split(ucat[...])
    total = jnp.zeros((2 * BLK, width), F32)
    for k in range(4):
        f_high, f_low = split(jnp.concatenate([fall[k, 0], fall[k, 1]], axis=0))
        at = slice(2 * k * BLK, 2 * (k + 1) * BLK)
        total = total + dot3(u_high[:, at], u_low[:, at], f_high, f_low)
    right[pl.ds(depth, 2 * BLK), :] = total
    off[...] = -2.0 * right[pl.ds(pl.multiple_of(depth + h * BLK, BLK), BLK), :]

    own = pltpu.make_async_copy(right.at[pl.ds(0, depth)], strips.at[slot, pl.ds(0, depth)], local.at[6])
    own_f = [
        pltpu.make_async_copy(fall.at[y, k], strips.at[slot, pl.ds(depth + k * BLK, BLK)], local.at[7 + k]) for k in range(2)
    ]

    @pl.when(source)
    def _():
        own.start()
        for copy in own_f:
            copy.start()
        own.wait()
        for copy in own_f:
            copy.wait()

    for s in spread_a + spread_f:

        @pl.when(source)
        def _(s=s):
            s[1].wait_recv()
            s[0].wait_send()
            s[1].wait_send()

        @pl.when(jnp.logical_not(source))
        def _(s=s):
            s[2].wait_recv()
            s[2].wait_send()

    @pl.when(top)
    def _():
        swap.wait()

    @pl.when(h == 1)
    def _():
        for copy in to_top:
            copy.wait_send()

    for copy in to_sibling + [f_out, f_back, u_swap]:
        copy.wait_send()
    for group in (lower_gather, rs_f, rs_p, rs_q, rs_r, ag_f, ag_u):
        group.drain()


def front(inverse, lower, tiles):
    depth, width = inverse.shape
    tall = depth + 2 * BLK
    vmem = lambda *shape: pltpu.VMEM(shape, F32)
    tile = (BLK, BLK)
    rows = (BLK, width)
    scratch = [
        vmem(4, 2, BLK, depth),
        pltpu.VMEM((depth, width), BF16),
        pltpu.VMEM((depth, width), BF16),
        vmem(4, 2, *rows),
        vmem(2, *rows),
        vmem(2, 2, *rows),
        vmem(*rows),
        vmem(2, *rows),
        vmem(4, 2, *rows),
        vmem(4, 2, 2, 2, 4, *tile),
        vmem(4, 2, 2, 2, 4, *tile),
        vmem(2, 2, 2, 4, *tile),
        vmem(2, 2, 2, 2, 4, *tile),
        vmem(4, 2, 4, *tile),
        vmem(2, 4, *tile),
        vmem(2, 2, 4, *tile),
        vmem(4, 2, *tile),
        vmem(2, *tile),
        vmem(2, 2, *tile),
        vmem(*tile),
        vmem(4, 2, *tile),
        vmem(4, 2, *tile),
        vmem(2 * BLK, 8 * BLK),
        pltpu.SemaphoreType.DMA((64,)),
        pltpu.SemaphoreType.DMA((64,)),
        pltpu.SemaphoreType.DMA((16,)),
    ]
    whole = pl.BlockSpec(memory_space=pltpu.VMEM)
    return pl.pallas_call(
        front_kernel,
        out_shape=(
            jax.ShapeDtypeStruct((2, tall, width), F32),
            jax.ShapeDtypeStruct((tall, width), F32),
            jax.ShapeDtypeStruct((depth, width), F32),
            jax.ShapeDtypeStruct((BLK, 2 * BLK), F32),
            jax.ShapeDtypeStruct((BLK, width), F32),
        ),
        in_specs=[whole, whole, pl.BlockSpec(memory_space=pl.ANY)],
        out_specs=(whole,) * 5,
        scratch_shapes=scratch,
        compiler_params=pltpu.CompilerParams(collective_id=0, has_side_effects=True, vmem_limit_bytes=67043328),
        name="front",
    )(inverse, lower.reshape(2, BLK, depth), tiles.reshape(2, 4, 2, 2, 2, 4, *tile))


def pivot_kernel(part, out, first, second, send, recv):
    _, _, _, _, _, y, _ = place()
    near = neighbours()
    ring = (near["yp"], near["ym"])
    rows = part.shape[2]
    rs = Scatter(Copies(send, recv), part, first, second, y, *ring, add_rows(rows, 32))
    greet(list(ring))
    rs.start()
    rs.middle()
    rs.arrived()
    for k in range(2):

        def body(i, _, k=k):
            at = pl.ds(pl.multiple_of(i * 32, 32), 32)
            to = pl.ds(pl.multiple_of(i * 32 + k * rows, 32), 32)
            out[to, :] = part[y, k, at, :] + second[0, k, at, :] + second[1, k, at, :]
            return 0

        lax.fori_loop(0, rows // 32, body, 0)
    rs.drain()


def pivot_sum(part):
    _, _, rows, width = part.shape
    whole = pl.BlockSpec(memory_space=pltpu.VMEM)
    return pl.pallas_call(
        pivot_kernel,
        out_shape=jax.ShapeDtypeStruct((2 * rows, width), F32),
        in_specs=[whole],
        out_specs=whole,
        scratch_shapes=[
            pltpu.VMEM((2, rows, width), F32),
            pltpu.VMEM((2, 2, rows, width), F32),
            pltpu.SemaphoreType.DMA((4,)),
            pltpu.SemaphoreType.DMA((4,)),
        ],
        compiler_params=pltpu.CompilerParams(collective_id=1, has_side_effects=True, vmem_limit_bytes=40 << 20),
        name="pivot_sum",
    )(part)


def shards(parent_adj, child_map, lower_panel, pivot_inverse):
    inverse, lower = pivot_inverse[0], lower_panel[0]
    tiles = select(child_map, parent_adj)
    strips, right, mate, update, off = front(inverse, lower, tiles)
    high = lax.Precision.HIGH
    product = lambda w, v: jnp.einsum("skn,km->snm", w, v, precision=high, preferred_element_type=F32)
    part = product(strips, right)
    _, _, _, row, h, _, z = place()

    def with_top(part):
        first = jnp.where(z == 0, inverse, mate)
        last = jnp.where(z == 0, mate, inverse)
        return part + product(jnp.stack([first, last]), inverse)

    part = lax.cond((h == 0) & (z < 2), with_top, lambda part: part, part)
    width = part.shape[2]
    pivot = pivot_sum(part.reshape(4, 2, width // 4, width))
    return (update[None], off[None], pivot[None])


def solution(mesh):
    in_specs = (P(("leaf", "row"), "col"), P(), P("leaf", "col", "row"), P("leaf", "row", "col"))
    out_specs = (P("leaf", "row", "col"), P("leaf", "row", "col"), P("leaf", "row", "col"))
    return jax.shard_map(shards, mesh=mesh, in_specs=in_specs, out_specs=out_specs, check_vma=False)
```

```python
import jax
import jax.numpy as jnp
from jax import lax
from jax.experimental import pallas as pl
from jax.experimental.pallas import tpu as pltpu
from jax.sharding import PartitionSpec as P

BLK = 128
MESH = pl.DeviceIdType.MESH
F32 = jnp.float32
BF16 = jnp.bfloat16


def split(a):
    high = a.astype(BF16)
    return high, (a - high.astype(F32)).astype(BF16)


def dot3(a_high, a_low, b_high, b_low):
    dot = lambda p, q: jnp.dot(p, q, preferred_element_type=F32)
    return dot(a_high, b_high) + (dot(a_high, b_low) + dot(a_low, b_high))


def place():
    leaf, row, col = lax.axis_index("leaf"), lax.axis_index("row"), lax.axis_index("col")
    return leaf, leaf // 2, leaf % 2, row, row // 4, row % 4, col


def neighbours():
    leaf, xl, _, row, h, y, z = place()
    return dict(
        zp=(leaf, row, (z + 1) % 4),
        zm=(leaf, row, (z + 3) % 4),
        yp=(leaf, h * 4 + (y + 1) % 4, z),
        ym=(leaf, h * 4 + (y + 3) % 4, z),
        xp=((leaf + 2) % 4, (row + 4 * xl) % 8, z),
        xm=((leaf + 2) % 4, (row + 4 * (1 - xl)) % 8, z),
        hx=(leaf, (row + 4) % 8, z),
        core=(xl * 2 + (1 - leaf % 2), row, z),
    )


class Copies:
    def __init__(self, send, recv):
        self.send, self.recv, self.count = send, recv, 0

    def make(self, src, dst, device):
        n = self.count
        self.count += 1
        return pltpu.make_async_remote_copy(
            src_ref=src, dst_ref=dst, send_sem=self.send.at[n], recv_sem=self.recv.at[n], device_id=device, device_id_type=MESH
        )


class Scatter:
    def __init__(self, copies, x, first, second, pos, plus, minus, add):
        self.x, self.first, self.second, self.pos, self.add = x, first, second, pos, add
        self.right, self.left, far = (pos + 1) % 4, (pos + 3) % 4, (pos + 2) % 4
        self.a = copies.make(x.at[far, 0], first.at[0], plus)
        self.b = copies.make(x.at[far, 1], first.at[1], minus)
        self.c = copies.make(x.at[self.right], second.at[0], plus)
        self.d = copies.make(x.at[self.left], second.at[1], minus)

    def start(self):
        self.a.start()
        self.b.start()

    def middle(self):
        self.a.wait_recv()
        self.add(self.x.at[self.right, 0], self.x.at[self.right, 0], self.first.at[0])
        self.c.start()
        self.b.wait_recv()
        self.add(self.x.at[self.left, 1], self.x.at[self.left, 1], self.first.at[1])
        self.d.start()

    def arrived(self):
        self.c.wait_recv()
        self.d.wait_recv()

    def drain(self):
        for copy in (self.a, self.b, self.c, self.d):
            copy.wait_send()


class Gather:
    def __init__(self, copies, x, pos, plus, minus, own=None):
        source = x.at[pos] if own is None else own
        right, left = (pos + 1) % 4, (pos + 3) % 4
        self.a = copies.make(source, x.at[pos], plus)
        self.b = copies.make(source, x.at[pos], minus)
        self.c = copies.make(x.at[left, 0], x.at[left, 0], plus)
        self.d = copies.make(x.at[right, 1], x.at[right, 1], minus)

    def start(self):
        self.a.start()
        self.b.start()

    def middle(self):
        self.a.wait_recv()
        self.c.start()
        self.b.wait_recv()
        self.d.start()

    def arrived(self):
        self.c.wait_recv()
        self.d.wait_recv()

    def drain(self):
        for copy in (self.a, self.b, self.c, self.d):
            copy.wait_send()


def greet(near):
    barrier = pltpu.get_barrier_semaphore()
    for device in near:
        pl.semaphore_signal(barrier, inc=1, device_id=device, device_id_type=MESH)
    pl.semaphore_wait(barrier, len(near))


def add_rows(count, step):
    def add(dst, a, b):
        def body(i, _):
            at = pl.ds(pl.multiple_of(i * step, step), step)
            dst[at, :] = a[at, :] + b[at, :]
            return 0

        lax.fori_loop(0, count // step, body, 0)

    return add


def add_tiles(dst, a, b):
    if len(dst.shape) == 2:
        dst[...] = a[...] + b[...]
        return

    def body(i, _):
        add_tiles(dst.at[i], a.at[i], b.at[i])
        return 0

    lax.fori_loop(0, dst.shape[0], body, 0)


def select_kernel(blocks, parent, out):
    leaf, _, core, row, _, _, z = place()
    owner = leaf * 8 + row
    step = pl.program_id(0)
    kind, y_to = step // 4, step % 4
    parity = jnp.where(kind == 0, core, 1 - core)

    def body(n, _):
        h_to, xl_to, j = n // 16, (n // 8) % 2, n % 8
        child = 2 * xl_to + parity
        r = blocks[child, 4 * h_to + y_to] - 4 * owner
        c = blocks[child, j] - 32 * z
        held = (r >= 0) & (r < 4) & (c >= 0) & (c < 32)
        r, c = jnp.clip(r, 0, 3), jnp.clip(c, 0, 31)
        tile = parent[pl.ds(pl.multiple_of(r * BLK, BLK), BLK), pl.ds(pl.multiple_of(c * BLK, BLK), BLK)]
        out[0, 0, n] = jnp.where(held, tile, 0.0)
        return 0

    lax.fori_loop(0, 32, body, 0)


def select(child_map, parent):
    return pl.pallas_call(
        select_kernel,
        grid=(8,),
        out_shape=jax.ShapeDtypeStruct((2, 4, 32, BLK, BLK), F32),
        in_specs=[
            pl.BlockSpec(memory_space=pltpu.SMEM),
            pl.BlockSpec(parent.shape, lambda s: (0, 0), pipeline_mode=pl.Buffered(1)),
        ],
        out_specs=pl.BlockSpec((1, 1, 32, BLK, BLK), lambda s: (s // 4, s % 4, 0, 0, 0)),
        compiler_params=pltpu.CompilerParams(vmem_limit_bytes=32 << 20),
        name="select",
    )(child_map, parent)


CHUNKS = 4


def front_kernel(
    inverse, lower, tiles,
    strips, right, mate, extra, update, off,
    lower_all, high, low, xf, f1, f2, fx, fpair, fall,
    sib, xp, p1, p2, xq, q1, q2, xr, r1, r2, held, uall, upair, ucat,
    send, recv, local,
):
    leaf, xl, core, row, h, y, z = place()
    near = neighbours()
    copies = Copies(send, recv)
    role = (z + 2 * h) % 4
    slot = ((role + 1) // 2) % 2
    even = z % 2 == 0
    pair = (leaf, row, jnp.where(even, (z + 1) % 4, (z + 3) % 4))
    cross = (leaf, row, jnp.where(even, (z + 3) % 4, (z + 1) % 4))
    source, upper = role < 2, h == 0
    top = source & upper
    depth, width = inverse.shape
    piece = depth // CHUNKS

    lower_gather = Gather(copies, lower_all, z, near["zp"], near["zm"], own=lower)
    to_sibling = [copies.make(tiles.at[1, (y + d) % 4], sib.at[(y + d) % 4], near["core"]) for d in (2, 1, 3, 0)]
    to_top = []
    for q in range(CHUNKS):
        at = pl.ds(q * piece, piece)
        to_top.append(copies.make(inverse.at[at], right.at[at], near["hx"]))
    swap = copies.make(inverse, mate, pair)
    rs_f = Scatter(copies, xf, f1, f2, y, near["yp"], near["ym"], add_rows(BLK, 32))
    rs_p = Scatter(copies, xp, p1, p2, y, near["yp"], near["ym"], add_tiles)
    rs_q = Scatter(copies, xq, q1, q2, 2 * h + xl, near["xp"], near["xm"], add_tiles)
    rs_r = Scatter(copies, xr, r1, r2, z, near["zp"], near["zm"], add_tiles)
    ag_f = Gather(copies, fall, y, near["yp"], near["ym"])
    ag_u = Gather(copies, uall, z, near["zp"], near["zm"])
    f_out = copies.make(fpair.at[1 - h], fx, near["hx"])
    f_back = copies.make(fall.at[y, h], fall.at[y, h], near["hx"])
    u_swap = copies.make(uall, upair, near["hx"])

    def spread(src, at_src, at):
        return (
            copies.make(src.at[at_src], strips.at[slot, at], cross),
            copies.make(src.at[at_src], strips.at[slot, at], pair),
            copies.make(strips.at[slot, at], strips.at[slot, at], pair),
        )

    spread_a = [spread(right, pl.ds(q * piece, piece), pl.ds(q * piece, piece)) for q in range(CHUNKS)]
    spread_f = [spread(fall.at[y, k], slice(None), pl.ds(depth + k * BLK, BLK)) for k in range(2)]

    def spread_start(s):
        s[0].start()
        s[1].start()

    def spread_forward(s):
        s[0].wait_recv()
        s[2].start()

    greet(list(near.values()))

    lower_here = pltpu.make_async_copy(lower, lower_all.at[z], local.at[0])
    lower_here.start()
    lower_gather.start()
    tiles_here = []
    for n, d in enumerate((2, 1, 3, 0)):
        to_sibling[n].start()
        copy = pltpu.make_async_copy(tiles.at[0, (y + d) % 4], xp.at[(y + d) % 4], local.at[1 + n])
        copy.start()
        tiles_here.append(copy)
    inverse_here = pltpu.make_async_copy(inverse, right.at[pl.ds(0, depth)], local.at[5])

    @pl.when(h == 1)
    def _():
        for copy in to_top:
            copy.start()
        inverse_here.start()

    @pl.when(top)
    def _():
        swap.start()

    def split_rows(i, _):
        at = pl.ds(pl.multiple_of(i * 32, 32), 32)
        high[at, :], low[at, :] = split(inverse[at, :])
        return 0

    lax.fori_loop(0, depth // 32, split_rows, 0)

    def sum_tiles(n):
        d = (2, 1, 3, 0)[n]
        tiles_here[n].wait()
        to_sibling[n].wait_recv()
        add_tiles(xp.at[(y + d) % 4], xp.at[(y + d) % 4], sib.at[(y + d) % 4])

    lower_gather.middle()
    sum_tiles(0)
    rs_p.start()
    lower_here.wait()
    lower_gather.arrived()

    def factor_rows(k, _):
        block = jnp.concatenate([lower_all[k, 0], lower_all[k, 1]], axis=0)
        a_high, a_low = split(block)
        product = dot3(a_high, a_low, high[...], low[...])
        xf[2 * (k % 2), k // 2] = product[:BLK]
        xf[2 * (k % 2) + 1, k // 2] = product[BLK:]
        return 0

    lax.fori_loop(0, 4, factor_rows, 0)
    rs_f.start()
    for n in (1, 2, 3):
        sum_tiles(n)
    rs_f.middle()
    rs_p.middle()

    @pl.when(h == 1)
    def _():
        inverse_here.wait()

    for q in range(CHUNKS):

        @pl.when(upper)
        def _(q=q):
            to_top[q].wait_recv()

        @pl.when(source)
        def _(q=q):
            spread_start(spread_a[q])

    @pl.when(top)
    def _():
        swap.wait_recv()
        cross_dot = lambda p, q: lax.dot_general(p, q, (((0,), (0,)), ((), ())), preferred_element_type=F32)

        def body(n, _):
            at = pl.ds(pl.multiple_of(n * 256, 256), 256)
            m_high, m_low = split(mate[:, at])
            for k, (to, w_high, w_low) in enumerate(((z, high[:, at], low[:, at]), (1 - z, m_high, m_low))):
                out = pltpu.make_async_copy(held.at[k], extra.at[to, at], local.at[9 + k])

                @pl.when(n > 0)
                def _():
                    out.wait()

                held[k] = cross_dot(w_high, high[...]) + (cross_dot(w_high, low[...]) + cross_dot(w_low, high[...]))
                out.start()
            return 0

        lax.fori_loop(0, width // 256, body, 0)

    rs_f.arrived()
    for k in range(2):
        add_rows(BLK, 32)(fpair.at[k], xf.at[y, k], f2.at[0, k])
        add_rows(BLK, 32)(fpair.at[k], fpair.at[k], f2.at[1, k])
    f_out.start()

    @pl.when(jnp.logical_not(source))
    def _():
        for s in spread_a:
            spread_forward(s)

    f_out.wait_recv()
    add_rows(BLK, 32)(fall.at[y, h], fpair.at[h], fx)
    f_back.start()
    f_back.wait_recv()
    ag_f.start()

    @pl.when(source)
    def _():
        for s in spread_f:
            spread_start(s)

    rs_p.arrived()
    for k in range(2):
        for x in range(2):
            for g in range(2):
                add_tiles(xq.at[2 * k + x, g], xp.at[y, k, x, g], p2.at[0, k, x, g])
                add_tiles(xq.at[2 * k + x, g], xq.at[2 * k + x, g], p2.at[1, k, x, g])
    rs_q.start()

    @pl.when(jnp.logical_not(source))
    def _():
        for s in spread_f:
            spread_forward(s)

    ag_f.middle()
    rs_q.middle()
    rs_q.arrived()
    here = 2 * h + xl
    for g in range(2):
        for k in range(4):
            xr[2 * g + k // 2, k % 2] = xq[here, g, k] + q2[0, g, k] + q2[1, g, k]
    rs_r.start()
    rs_r.middle()
    rs_r.arrived()
    for k in range(2):
        tile = xr[z, k] + r2[0, k] + r2[1, k]
        uall[z, k] = tile
        update[:, k * BLK : (k + 1) * BLK] = tile
    ag_u.start()
    ag_u.middle()
    ag_u.arrived()
    u_swap.start()
    u_swap.wait_recv()
    ag_f.arrived()
    for j in range(8):
        to = (2 * (j % 4) + j // 4) * BLK
        ucat[pl.ds(pl.multiple_of(h * BLK, BLK), BLK), to : to + BLK] = uall[j // 2, j % 2]
        ucat[pl.ds(pl.multiple_of((1 - h) * BLK, BLK), BLK), to : to + BLK] = upair[j // 2, j % 2]

    u_high, u_low = split(ucat[...])
    total = jnp.zeros((2 * BLK, width), F32)
    for k in range(4):
        f_high, f_low = split(jnp.concatenate([fall[k, 0], fall[k, 1]], axis=0))
        at = slice(2 * k * BLK, 2 * (k + 1) * BLK)
        total = total + dot3(u_high[:, at], u_low[:, at], f_high, f_low)
    right[pl.ds(depth, 2 * BLK), :] = total
    off[...] = -2.0 * right[pl.ds(pl.multiple_of(depth + h * BLK, BLK), BLK), :]

    own = pltpu.make_async_copy(right.at[pl.ds(0, depth)], strips.at[slot, pl.ds(0, depth)], local.at[6])
    own_f = [
        pltpu.make_async_copy(fall.at[y, k], strips.at[slot, pl.ds(depth + k * BLK, BLK)], local.at[7 + k]) for k in range(2)
    ]

    @pl.when(source)
    def _():
        own.start()
        for copy in own_f:
            copy.start()
        own.wait()
        for copy in own_f:
            copy.wait()

    for s in spread_a + spread_f:

        @pl.when(source)
        def _(s=s):
            s[1].wait_recv()
            s[0].wait_send()
            s[1].wait_send()

        @pl.when(jnp.logical_not(source))
        def _(s=s):
            s[2].wait_recv()
            s[2].wait_send()

    @pl.when(top)
    def _():
        swap.wait_send()
        for k in range(2):
            pltpu.make_async_copy(held.at[k], extra.at[k, pl.ds(0, 256)], local.at[9 + k]).wait()

    @pl.when(h == 1)
    def _():
        for copy in to_top:
            copy.wait_send()

    for copy in to_sibling + [f_out, f_back, u_swap]:
        copy.wait_send()
    for group in (lower_gather, rs_f, rs_p, rs_q, rs_r, ag_f, ag_u):
        group.drain()


def front(inverse, lower, tiles):
    depth, width = inverse.shape
    tall = depth + 2 * BLK
    vmem = lambda *shape: pltpu.VMEM(shape, F32)
    tile = (BLK, BLK)
    rows = (BLK, width)
    scratch = [
        vmem(4, 2, BLK, depth),
        pltpu.VMEM((depth, width), BF16),
        pltpu.VMEM((depth, width), BF16),
        vmem(4, 2, *rows),
        vmem(2, *rows),
        vmem(2, 2, *rows),
        vmem(*rows),
        vmem(2, *rows),
        vmem(4, 2, *rows),
        vmem(4, 2, 2, 2, 4, *tile),
        vmem(4, 2, 2, 2, 4, *tile),
        vmem(2, 2, 2, 4, *tile),
        vmem(2, 2, 2, 2, 4, *tile),
        vmem(4, 2, 4, *tile),
        vmem(2, 4, *tile),
        vmem(2, 2, 4, *tile),
        vmem(4, 2, *tile),
        vmem(2, *tile),
        vmem(2, 2, *tile),
        vmem(2, 256, width),
        vmem(4, 2, *tile),
        vmem(4, 2, *tile),
        vmem(2 * BLK, 8 * BLK),
        pltpu.SemaphoreType.DMA((64,)),
        pltpu.SemaphoreType.DMA((64,)),
        pltpu.SemaphoreType.DMA((16,)),
    ]
    whole = pl.BlockSpec(memory_space=pltpu.VMEM)
    return pl.pallas_call(
        front_kernel,
        out_shape=(
            jax.ShapeDtypeStruct((2, tall, width), F32),
            jax.ShapeDtypeStruct((tall, width), F32),
            jax.ShapeDtypeStruct((depth, width), F32),
            jax.ShapeDtypeStruct((2, width, width), F32),
            jax.ShapeDtypeStruct((BLK, 2 * BLK), F32),
            jax.ShapeDtypeStruct((BLK, width), F32),
        ),
        in_specs=[whole, whole, pl.BlockSpec(memory_space=pl.ANY)],
        out_specs=(whole,) * 3 + (pl.BlockSpec(memory_space=pl.ANY),) + (whole,) * 2,
        scratch_shapes=scratch,
        compiler_params=pltpu.CompilerParams(collective_id=0, has_side_effects=True, vmem_limit_bytes=67043328),
        name="front",
    )(inverse, lower.reshape(2, BLK, depth), tiles.reshape(2, 4, 2, 2, 2, 4, *tile))


def pivot_kernel(part, out, first, second, send, recv):
    _, _, _, _, _, y, _ = place()
    near = neighbours()
    ring = (near["yp"], near["ym"])
    rows = part.shape[2]
    rs = Scatter(Copies(send, recv), part, first, second, y, *ring, add_rows(rows, 32))
    greet(list(ring))
    rs.start()
    rs.middle()
    rs.arrived()
    for k in range(2):

        def body(i, _, k=k):
            at = pl.ds(pl.multiple_of(i * 32, 32), 32)
            to = pl.ds(pl.multiple_of(i * 32 + k * rows, 32), 32)
            out[to, :] = part[y, k, at, :] + second[0, k, at, :] + second[1, k, at, :]
            return 0

        lax.fori_loop(0, rows // 32, body, 0)
    rs.drain()


def pivot_sum(part):
    _, _, rows, width = part.shape
    whole = pl.BlockSpec(memory_space=pltpu.VMEM)
    return pl.pallas_call(
        pivot_kernel,
        out_shape=jax.ShapeDtypeStruct((2 * rows, width), F32),
        in_specs=[whole],
        out_specs=whole,
        scratch_shapes=[
            pltpu.VMEM((2, rows, width), F32),
            pltpu.VMEM((2, 2, rows, width), F32),
            pltpu.SemaphoreType.DMA((4,)),
            pltpu.SemaphoreType.DMA((4,)),
        ],
        compiler_params=pltpu.CompilerParams(collective_id=1, has_side_effects=True, vmem_limit_bytes=40 << 20),
        name="pivot_sum",
    )(part)


def shards(parent_adj, child_map, lower_panel, pivot_inverse):
    inverse, lower = pivot_inverse[0], lower_panel[0]
    tiles = select(child_map, parent_adj)
    strips, right, _, extra, update, off = front(inverse, lower, tiles)
    part = jnp.einsum("skn,km->snm", strips, right, precision=lax.Precision.HIGH, preferred_element_type=F32)
    _, _, _, _, h, _, z = place()
    part = part + jnp.where((h == 0) & (z < 2), extra, 0.0)
    width = part.shape[2]
    pivot = pivot_sum(part.reshape(4, 2, width // 4, width))
    return (update[None], off[None], pivot[None])


def solution(mesh):
    in_specs = (P(("leaf", "row"), "col"), P(), P("leaf", "col", "row"), P("leaf", "row", "col"))
    out_specs = (P("leaf", "row", "col"), P("leaf", "row", "col"), P("leaf", "row", "col"))
    return jax.shard_map(shards, mesh=mesh, in_specs=in_specs, out_specs=out_specs, check_vma=False)
```
